128 devices in a mesh: mem: 4 (over y), brick: 32 (over z, x, core).
Axes of the slice: x: 4, y: 4, z: 4, core: 2. Of those that a mesh axis runs over, the one named last changes fastest.
Arguments:
- members: float32 [128, 524288], P('mem', 'brick'), may hold values from -6 to 6
- predicted: float32 [128, 40, 4096], P('brick', None, 'mem'), may hold values from -6 to 6
- perturbation: float32 [128, 40, 4096], P('brick', None, 'mem'), may hold values from -6 to 6
- observed: float32 [40, 4096], P(None, ('mem', 'brick')), may hold values from -6 to 6
- noise_std: float32 [40, 4096], P(None, ('mem', 'brick')), may hold values from 0.3 to 3
- taper_weights: bfloat16 [4096, 512], P(('mem', 'brick')), may hold values from 0.099609375 to 1
- foot_brick: int32 [4096, 1], P(('mem', 'brick')), may hold values from 0 to 31; in each aligned block of 32 rows (0 to 31, 32 to 63, ...) at most 2 rows name the same one
- foot_tiles: int32 [4096, 4], P(('mem', 'brick')), may hold values from 0 to 127
Outputs:
- updated: float32 [128, 524288], P('mem', 'brick')
The draws below stay inside these ranges and needn't reach their ends.
Inputs may be any that keep to these rules, and one draw needn't show every extreme that they name: `foot_brick`: among the 32 soundings of one owner (aligned blocks of rows) at most 2 have their footprint in one brick, and some brick receives exactly 2 from some owner in every draw. `foot_tiles`: tile numbers inside the sounding's brick.
All inputs are finite; a program needn't handle non-finite values.
Results may differ from the reference program's by a relative error of at most 0.012.
Values may be sent and summed in bfloat16 or wider, within the bound.
No kernel may reach another device: no remote copies, remote signals or barrier semaphores. Data moves between devices by JAX's collectives and lax.ppermute only.
A program may use at most 64 MiB of HBM per device.

```python
import math
import jax
import jax.numpy as jnp
import numpy as np
from jax import lax

ENS = 128
GATES = 40
FT = 4
SND_DEV = 32
CELLS = 16384
CAP = 2
TILES = 128
SOUNDINGS = 4096
NCELLS = 524288
N_BRICK = 32


def set_ends(drawn, stream_key, low, top_value):
    longest = drawn.shape.index(max(drawn.shape))
    spots = []
    for shift in (0, 1):
        where = [jax.random.randint(jax.random.fold_in(stream_key, axis), (), 0, length) for axis, length in enumerate(drawn.shape)]
        where[longest] = (where[longest] + shift) % drawn.shape[longest]
        spots.append(tuple(where))
    return drawn.at[spots[0]].set(low).at[spots[1]].set(top_value)


def block_scale(key, extent, shards, least, largest):
    loudness = 1.0
    for dim, parts in shards:
        steps = jax.random.uniform(jax.random.fold_in(jax.random.fold_in(key, 6), dim), (parts,), jnp.float32, least / len(shards), largest / len(shards))
        loudness = loudness * jnp.repeat(jnp.exp(steps), extent[dim] // parts).reshape((-1,) + (1,) * (len(extent) - 1 - dim))
    return loudness


def routed_block(own_key, own, number, rows, count, top, limit, slope):
    sequence = jax.random.permutation(own_key, count)
    crowded, ordinary = load_shares(count, rows * top, limit, slope, True), load_shares(count, rows * top, limit, slope, False)
    places = jnp.arange(count)

    def named(sizes, turn):
        used = int((sizes > 0).sum())
        fixed = max(1, used // 4)
        passed = fixed + (places - fixed + turn * (used - fixed)) % max(1, count - fixed)
        return jnp.zeros((count,), jnp.int32).at[sequence[jnp.where(places < fixed, places, passed)]].set(jnp.asarray(sizes, jnp.int32))

    sizes = jnp.where(number % 4 == 0, named(crowded, number // 4), named(ordinary, number - number // 4 - 1))
    mixed = jax.random.permutation(jax.random.fold_in(own, 3), count)
    source_of, sink = mixed[0:count // 2 * 2:2], mixed[1:count // 2 * 2:2]
    room = jnp.minimum(sizes[source_of] - 1, limit - sizes[sink]) // 2
    room = jnp.where((source_of == sequence[0]) | (sink == sequence[0]) | (sizes[sink] == 0), 0, jnp.maximum(room, 0))
    passed = jax.random.randint(jax.random.fold_in(own, 4), (count // 2,), 0, 1 << 20) % (room + 1)
    sizes = sizes.at[source_of].add(-passed).at[sink].add(passed)
    labels = jnp.searchsorted(jnp.cumsum(sizes), jnp.arange(rows * top), side="right").astype(jnp.int32)
    table = labels.reshape(top, rows).T
    table = table[jax.random.permutation(jax.random.fold_in(own, 1), rows)]
    turn = jax.random.randint(jax.random.fold_in(own, 2), (rows, 1), 0, top)
    return jnp.take_along_axis(table, (jnp.arange(top)[None, :] + turn) % top, axis=1)


def load_shares(number_of, total, bound, lean, full):
    weights = [(1 << 20) // math.isqrt(standing ** lean) + 1 for standing in range(1, number_of + 1)]
    largest = bound if full else min(bound, max(-(-total // number_of), total * weights[0] // sum(weights)))
    least = 1 if total - largest >= number_of - 1 else 0
    holding, spare = [largest] + [least] * (number_of - 1), total - largest - least * (number_of - 1)
    while spare > 0:
        free = [i for i in range(1, number_of) if holding[i] < largest] or [i for i in range(1, number_of) if holding[i] < bound]
        mass, remaining = sum([weights[i] for i in free]), spare
        for i in free:
            more = min(bound - holding[i], max(1, remaining * weights[i] // mass), spare)
            holding[i] = holding[i] + more
            spare = spare - more
    return np.array(holding)


def noise(own_key, shape, spread, limit, cuts=(), kind=jnp.bfloat16):
    factor_of = block_scale(own_key, shape, cuts, -0.22, 0.18) if cuts else 1.0
    result = jax.random.normal(own_key, shape, jnp.float32) * spread * factor_of
    return jnp.minimum(jnp.maximum(result, -limit), limit).astype(kind)


def setup_inputs(seed: int = 0) -> dict:
    splits = jax.random.split(jax.random.key(seed), 9)
    members = noise(splits[0], (ENS, NCELLS), 1.0, 6.0, ((0, 4), (1, 32)), jnp.float32)
    predicted = noise(splits[1], (ENS, GATES, SOUNDINGS), 1.0, 6.0, ((0, 32), (2, 4)), jnp.float32)
    perturbation = noise(splits[2], (ENS, GATES, SOUNDINGS), 1.0, 6.0, ((0, 32), (2, 4)), jnp.float32)
    observed = noise(splits[3], (GATES, SOUNDINGS), 1.0, 6.0, ((1, 128),), jnp.float32)
    noise_std = jnp.clip(jnp.exp(math.log(3.0) - 2.3025851 * jax.random.uniform(splits[4], (GATES, SOUNDINGS), jnp.float32) ** block_scale(splits[4], (GATES, SOUNDINGS), ((1, 128),), -0.2, 0.2)), 0.3, 3.0)
    taper_weights = jnp.clip(0.099609375 + 0.9003906 * jax.random.uniform(splits[5], (SOUNDINGS, FT * 128), jnp.float32) ** block_scale(splits[5], (SOUNDINGS, FT * 128), ((0, 128),), -0.2, 0.2), 0.099609375, 1.0).astype(jnp.bfloat16)
    foot_brick_keys = jax.random.split(jax.random.fold_in(splits[6], 1), SOUNDINGS // SND_DEV)
    foot_brick_turns = jax.random.permutation(jax.random.fold_in(splits[6], 3), SOUNDINGS // SND_DEV)
    foot_brick = jax.vmap(lambda own, number: routed_block(jax.random.fold_in(splits[6], 2), own, number, SND_DEV, N_BRICK, 1, CAP, 2))(foot_brick_keys, foot_brick_turns).reshape((SOUNDINGS, 1))
    foot_tiles = set_ends(jax.random.randint(splits[7], (SOUNDINGS, FT), 0, CELLS // 128), jax.random.fold_in(splits[7], 1), 0, (CELLS // 128) - 1).astype(jnp.int32)
    return {"members": members, "predicted": predicted, "perturbation": perturbation, "observed": observed, "noise_std": noise_std, "taper_weights": taper_weights, "foot_brick": foot_brick, "foot_tiles": foot_tiles}


def owner_factors(predicted, perturbation, observed, noise_std):
    ensemble = predicted.shape[0]
    gate_count = predicted.shape[1]
    gate_mean = jnp.mean(predicted, axis=0)
    anomaly = predicted - gate_mean[None]
    covariance = jnp.einsum('jgs,jhs->sgh', anomaly, anomaly, precision=lax.Precision.HIGHEST) / (ensemble - 1.0)
    variance = jnp.transpose(noise_std * noise_std)
    covariance = covariance + variance[:, :, None] * jnp.eye(gate_count, dtype=jnp.float32)[None]
    misfit = observed[None] + noise_std[None] * perturbation - predicted
    lower = jnp.linalg.cholesky(covariance)
    right_side = jnp.transpose(misfit, (2, 1, 0))
    halfway = jax.scipy.linalg.solve_triangular(lower, right_side, lower=True)
    solved = jax.scipy.linalg.solve_triangular(lower, halfway, lower=True, trans=1) / (ensemble - 1.0)
    gain_rows = jnp.transpose(solved, (0, 2, 1)).astype(jnp.bfloat16)
    anomaly_rows = jnp.transpose(anomaly, (2, 0, 1)).astype(jnp.bfloat16)
    return (anomaly_rows, gain_rows)

def reference(members, predicted, perturbation, observed, noise_std, taper_weights, foot_brick, foot_tiles):
    anomaly_rows, gain_rows = owner_factors(predicted, perturbation, observed, noise_std)
    tile_count = members.shape[1] // 128
    model_tiles = members.astype(jnp.bfloat16).reshape(ENS, tile_count, 128)
    global_tiles = (foot_brick[:, 0:1] * TILES + foot_tiles).astype(jnp.int32)
    block_size = math.gcd(SOUNDINGS, 256)
    step_count = SOUNDINGS // block_size

    def one_block(accumulated, pieces):
        anomaly_block, gain_block, taper_block, tile_block = pieces
        flat_tiles = tile_block.reshape(-1)
        gathered = model_tiles[:, flat_tiles].reshape(ENS, block_size, FT * 128)
        gate_field = jnp.einsum('bjg,jbp->bgp', anomaly_block.astype(jnp.float32), gathered.astype(jnp.float32), precision=lax.Precision.HIGHEST)
        gate_field = gate_field.astype(jnp.bfloat16)
        contribution = jnp.einsum('bjg,bgp->jbp', gain_block.astype(jnp.float32), gate_field.astype(jnp.float32), precision=lax.Precision.HIGHEST)
        contribution = contribution * taper_block.astype(jnp.float32)[None]
        accumulated = accumulated.at[:, flat_tiles].add(contribution.reshape(ENS, block_size * FT, 128))
        return (accumulated, None)
    start = jnp.zeros((ENS, tile_count, 128), jnp.float32)
    stacked = (anomaly_rows.reshape(step_count, block_size, ENS, GATES), gain_rows.reshape(step_count, block_size, ENS, GATES), taper_weights.reshape(step_count, block_size, FT * 128), global_tiles.reshape(step_count, block_size, FT))
    accumulated, _ = lax.scan(one_block, start, stacked)
    return members + accumulated.reshape(members.shape)
```

```python
import jax
import jax.numpy as jnp
from jax import lax
from jax.experimental import pallas as pl
from jax.experimental.pallas import tpu as pltpu
from jax.sharding import PartitionSpec as P

F32 = jnp.float32
BF16 = jnp.bfloat16
VMEM_LIMIT = 56 * 1024 * 1024
LANES = 128


def slot_of(brick_ref, count_ref, s, capacity):
    dest = brick_ref[s]
    rank = jnp.minimum(count_ref[dest], capacity - 1)
    count_ref[dest] = rank + 1
    return dest * capacity + rank


def pack_kernel(brick_ref, pred_ref, pert_ref, out_ref, *, part):
    members, gates, width = pred_ref.shape
    per_tile = LANES // part
    lane = lax.broadcasted_iota(jnp.int32, (gates, LANES), 1) // part
    for which, ref in enumerate((pred_ref, pert_ref)):
        for tile in range(width // LANES):
            blocks = [ref[j, :, tile * LANES : (tile + 1) * LANES] for j in range(members)]
            for q in range(per_tile):
                acc = None
                for j in range(members):
                    shift = ((j - q) * part) % LANES
                    moved = pltpu.roll(blocks[j], shift, 1) if shift else blocks[j]
                    acc = moved if acc is None else jnp.where(lane == j, moved, acc)
                out_ref[tile * per_tile + q, which * gates : (which + 1) * gates, :] = acc.astype(
                    BF16
                )


def taper_kernel(brick_ref, taper_ref, tiles_ref, out_ref, rows_ref, slots_ref, count_ref):
    soundings, length = taper_ref.shape
    pieces = length // LANES
    bricks = out_ref.shape[0] // (out_ref.shape[0] // count_ref.shape[0])
    rows_ref[...] = jnp.zeros_like(rows_ref)
    slots_ref[...] = jnp.zeros_like(slots_ref)
    for f in range(pieces):
        rows_ref[pl.ds(f, soundings, stride=8), :] = taper_ref[
            :, f * LANES : (f + 1) * LANES
        ].astype(F32)
    rows_ref[pl.ds(pieces, soundings, stride=8), :] = tiles_ref[...]
    capacity = slots_ref.shape[0] // bricks

    def clear(i, _):
        count_ref[i] = 0
        return 0

    lax.fori_loop(0, bricks, clear, 0)

    def place(s, _):
        slot = slot_of(brick_ref, count_ref, s, capacity)
        slots_ref[slot] = rows_ref[pl.ds(pl.multiple_of(s * 8, 8), 8), :]
        return 0

    lax.fori_loop(0, soundings, place, 0)
    packed = slots_ref[...].reshape(bricks, 8 * capacity, LANES).astype(BF16)
    for m in range(out_ref.shape[0] // bricks):
        out_ref[m * bricks : (m + 1) * bricks] = packed


def anomaly_kernel(
    brick_ref, got_ref, send_ref, pred_ref, pert_ref, wide_ref, turned_ref, slots_ref, count_ref
):
    sources = got_ref.shape[0]
    rows = got_ref.shape[1]
    gates = rows // 2
    soundings = pred_ref.shape[0]
    per_lane = LANES // soundings
    wide_ref[...] = got_ref[...].reshape(sources * rows, LANES).astype(F32)
    depth = per_lane * LANES
    r = lax.broadcasted_iota(jnp.int32, (depth, depth), 0)
    c = lax.broadcasted_iota(jnp.int32, (depth, depth), 1)
    want = (
        (c // LANES) * sources + ((c % LANES) // per_lane) + (c % per_lane) * LANES
    )
    select = jnp.where(r == want, 1.0, 0.0).astype(BF16)
    lefts = []
    for group in range(rows // per_lane):
        stack = jnp.concatenate(
            [
                wide_ref[pl.ds(group * per_lane + k, sources, stride=rows), :]
                for k in range(per_lane)
            ],
            axis=0,
        )
        turned = stack.T
        lefts.append(
            jnp.concatenate(
                [turned[j * soundings : (j + 1) * soundings, :] for j in range(per_lane)], axis=1
            ).astype(BF16)
        )
    left = jnp.concatenate(lefts, axis=0)
    placed = jnp.dot(left, select, preferred_element_type=F32)
    for group in range(rows // per_lane):
        for k in range(per_lane):
            g = group * per_lane + k
            block = placed[
                group * soundings : (group + 1) * soundings, k * LANES : (k + 1) * LANES
            ]
            if g < gates:
                turned_ref[0, pl.ds(g, soundings, stride=gates), :] = block
            else:
                turned_ref[1, pl.ds(g - gates, soundings, stride=gates), :] = block
    pred = turned_ref[0].reshape(soundings, gates, LANES)
    pred_ref[...] = pred
    pert_ref[...] = turned_ref[1].reshape(soundings, gates, LANES)
    bricks = count_ref.shape[0]
    capacity = slots_ref.shape[0] // bricks
    slots_ref[...] = jnp.zeros_like(slots_ref)

    def clear(i, _):
        count_ref[i] = 0
        return 0

    lax.fori_loop(0, bricks, clear, 0)

    def place(s, _):
        slot = slot_of(brick_ref, count_ref, s, capacity)
        one = pred_ref[s]
        mean = jnp.sum(one, axis=1, keepdims=True) * (1.0 / LANES)
        slots_ref[slot] = one - mean
        return 0

    lax.fori_loop(0, soundings, place, 0, unroll=4)
    packed = slots_ref[...].reshape(bricks, capacity * gates, LANES).astype(BF16)
    for m in range(send_ref.shape[0] // bricks):
        send_ref[m * bricks : (m + 1) * bricks] = packed


def gain_kernel(
    brick_ref, pred_ref, pert_ref, observed_ref, noise_ref, send_ref, slots_ref, count_ref
):
    soundings, gates, ensemble = pred_ref.shape
    bricks = count_ref.shape[0]
    capacity = slots_ref.shape[0] // bricks
    mems = send_ref.shape[0] // bricks
    block = ensemble // mems
    scale = 1.0 / (ensemble - 1.0)
    slots_ref[...] = jnp.zeros_like(slots_ref)

    def clear(i, _):
        count_ref[i] = 0
        return 0

    lax.fori_loop(0, bricks, clear, 0)
    row = lax.broadcasted_iota(jnp.int32, (gates, LANES), 0)
    lane = lax.broadcasted_iota(jnp.int32, (gates, LANES), 1)
    sub = lax.broadcasted_iota(jnp.int32, (gates, 1), 0)
    head = lax.broadcasted_iota(jnp.int32, (1, LANES), 1)
    unit = 8
    for first in range(0, soundings, unit):
        mats = []
        rights = []
        for s in range(first, first + unit):
            pred = pred_ref[s]
            mean = jnp.sum(pred, axis=1, keepdims=True) * (1.0 / ensemble)
            anomaly = pred - mean
            full = jnp.concatenate(
                [anomaly, jnp.zeros((LANES - gates, ensemble), F32)], axis=0
            )
            cov = lax.dot_general(
                anomaly,
                full,
                (((1,), (1,)), ((), ())),
                precision=lax.Precision.HIGHEST,
                preferred_element_type=F32,
            )
            noise = noise_ref[:, s : s + 1]
            mats.append(cov * scale + jnp.where(row == lane, noise * noise, 0.0))
            rights.append(observed_ref[:, s : s + 1] + noise * pert_ref[s] - pred)
        for k in range(gates):
            for u in range(unit):
                w = mats[u]
                inv = 1.0 / w[k : k + 1, k : k + 1]
                top = jnp.where(head == k, 1.0, w[k : k + 1, :]) * inv
                side = jnp.where(sub == k, -1.0, w[:, k : k + 1])
                kept = jnp.where((lane == k) | (row == k), 0.0, w)
                mats[u] = kept - side * top
        for u in range(unit):
            s = first + u
            solved = (
                jnp.dot(
                    mats[u][:, :gates],
                    rights[u],
                    precision=lax.Precision.HIGHEST,
                    preferred_element_type=F32,
                )
                * scale
            )
            slot = slot_of(brick_ref, count_ref, s, capacity)
            slots_ref[slot, 0:gates, :] = solved
    for d in range(bricks):
        stack = slots_ref[d * capacity : (d + 1) * capacity].reshape(LANES, ensemble)
        turned = stack.T.astype(BF16)
        for m in range(mems):
            send_ref[m * bricks + d] = turned[m * block : (m + 1) * block, :]


def update_kernel(
    tiles_ref, model_ref, anomaly_ref, gain_ref, taper_ref, members_ref, out_ref, *, unit
):
    sources, rows, ensemble = anomaly_ref.shape
    capacity = taper_ref.shape[1] // 8
    gates = rows // capacity
    pieces = tiles_ref.shape[0] // (sources * capacity)
    span = LANES // capacity
    out_ref[...] = members_ref[...]

    def turn(i, _):
        work = []
        for u in range(unit):
            src = i * unit + u
            anomalies = anomaly_ref[src]
            gains = gain_ref[src]
            tapers = taper_ref[src].astype(F32)
            for c in range(capacity):
                where = [
                    pl.multiple_of(tiles_ref[(src * capacity + c) * pieces + f] * LANES, LANES)
                    for f in range(pieces)
                ]
                cells = jnp.concatenate(
                    [model_ref[:, pl.ds(at, LANES)] for at in where], axis=1
                )
                field = jnp.dot(
                    anomalies[c * gates : (c + 1) * gates, :], cells, preferred_element_type=F32
                ).astype(BF16)
                rise = jnp.dot(
                    gains[:, c * span : c * span + gates], field, preferred_element_type=F32
                )
                work.append((where, rise, tapers[8 * c : 8 * c + pieces, :]))
        for where, rise, taper in work:
            for f in range(pieces):
                at = pl.ds(where[f], LANES)
                out_ref[:, at] = (
                    out_ref[:, at]
                    + rise[:, f * LANES : (f + 1) * LANES] * taper[f : f + 1, :]
                )
        return 0

    lax.fori_loop(0, sources // unit, turn, 0)


def params():
    return pltpu.CompilerParams(vmem_limit_bytes=VMEM_LIMIT)


def vmem(n):
    return [pl.BlockSpec(memory_space=pltpu.VMEM)] * n


def smem():
    return pl.BlockSpec(memory_space=pltpu.SMEM)


def body(
    members, predicted, perturbation, observed, noise_std, taper_weights, foot_brick, foot_tiles
):
    mems = lax.axis_size("mem")
    bricks = lax.axis_size("brick")
    devices = mems * bricks
    gates = predicted.shape[1]
    soundings = observed.shape[1]
    ensemble = predicted.shape[0] * bricks
    capacity = 2
    slots = bricks * capacity
    pieces = foot_tiles.shape[1]
    brick = foot_brick[:, 0]
    sds = jax.ShapeDtypeStruct

    model_all = lax.all_gather(members.astype(BF16), "mem", axis=0, tiled=True)

    packed = pl.pallas_call(
        lambda *refs: pack_kernel(*refs, part=soundings),
        out_shape=sds((bricks, 2 * gates, LANES), BF16),
        in_specs=[smem()] + vmem(2),
        out_specs=vmem(1)[0],
        compiler_params=params(),
        name="pack",
    )(brick, predicted, perturbation)
    got = lax.all_to_all(packed, "brick", split_axis=0, concat_axis=0, tiled=True)

    tile_rows = jnp.pad(foot_tiles.astype(F32), ((0, 0), (0, LANES - pieces)))
    taper_send = pl.pallas_call(
        taper_kernel,
        out_shape=sds((devices, 8 * capacity, LANES), BF16),
        in_specs=[smem()] + vmem(2),
        out_specs=vmem(1)[0],
        scratch_shapes=[
            pltpu.VMEM((soundings * 8, LANES), F32),
            pltpu.VMEM((slots, 8, LANES), F32),
            pltpu.SMEM((bricks,), jnp.int32),
        ],
        compiler_params=params(),
        name="route_taper",
    )(brick, taper_weights, tile_rows)
    taper_recv = lax.all_to_all(
        taper_send, ("mem", "brick"), split_axis=0, concat_axis=0, tiled=True
    )
    tiles = (
        taper_recv.reshape(devices, capacity, 8, LANES)[:, :, pieces, :pieces]
        .astype(jnp.int32)
        .reshape(devices * capacity * pieces)
    )

    anomaly_send, pred, pert = pl.pallas_call(
        anomaly_kernel,
        out_shape=(
            sds((devices, capacity * gates, LANES), BF16),
            sds((soundings, gates, ensemble), F32),
            sds((soundings, gates, ensemble), F32),
        ),
        in_specs=[smem()] + vmem(1),
        out_specs=tuple(vmem(3)),
        scratch_shapes=[
            pltpu.VMEM((bricks * 2 * gates, LANES), F32),
            pltpu.VMEM((2, soundings * gates, LANES), F32),
            pltpu.VMEM((slots, gates, LANES), F32),
            pltpu.SMEM((bricks,), jnp.int32),
        ],
        compiler_params=params(),
        name="anomaly",
    )(brick, got)
    anomaly_recv = lax.all_to_all(
        anomaly_send, ("mem", "brick"), split_axis=0, concat_axis=0, tiled=True
    )
    gain_send = pl.pallas_call(
        gain_kernel,
        out_shape=sds((devices, ensemble // mems, LANES), BF16),
        in_specs=[smem()] + vmem(4),
        out_specs=vmem(1)[0],
        scratch_shapes=[
            pltpu.VMEM((slots, LANES // capacity, ensemble), F32),
            pltpu.SMEM((bricks,), jnp.int32),
        ],
        compiler_params=params(),
        name="gain",
    )(brick, pred, pert, observed, noise_std)
    gain_recv = lax.all_to_all(
        gain_send, ("mem", "brick"), split_axis=0, concat_axis=0, tiled=True
    )
    return pl.pallas_call(
        lambda *refs: update_kernel(*refs, unit=2),
        out_shape=sds(members.shape, F32),
        in_specs=[smem()] + vmem(5),
        out_specs=vmem(1)[0],
        compiler_params=params(),
        name="update",
    )(tiles, model_all, anomaly_recv, gain_recv, taper_recv, members)


def solution(mesh):
    in_specs = (
        P("mem", "brick"),
        P("brick", None, "mem"),
        P("brick", None, "mem"),
        P(None, ("mem", "brick")),
        P(None, ("mem", "brick")),
        P(("mem", "brick"), None),
        P(("mem", "brick"), None),
        P(("mem", "brick"), None),
    )
    out_specs = P("mem", "brick")
    return jax.shard_map(body, mesh=mesh, in_specs=in_specs, out_specs=out_specs, check_vma=False)
```

```python
import jax
import jax.numpy as jnp
from jax import lax
from jax.experimental import pallas as pl
from jax.experimental.pallas import tpu as pltpu
from jax.sharding import PartitionSpec as P

F32 = jnp.float32
BF16 = jnp.bfloat16
VMEM_LIMIT = 56 * 1024 * 1024
LANES = 128


def slot_of(brick_ref, count_ref, s, capacity):
    dest = brick_ref[s]
    rank = jnp.minimum(count_ref[dest], capacity - 1)
    count_ref[dest] = rank + 1
    return dest * capacity + rank


def clear_counts(count_ref):
    def clear(i, _):
        count_ref[i] = 0
        return 0

    lax.fori_loop(0, count_ref.shape[0], clear, 0)


def pack_kernel(pred_ref, pert_ref, out_ref, *, part):
    members, gates, width = pred_ref.shape
    per_tile = LANES // part
    lane = lax.broadcasted_iota(jnp.int32, (gates, LANES), 1) // part
    for which, ref in enumerate((pred_ref, pert_ref)):
        for tile in range(width // LANES):
            blocks = [ref[j, :, tile * LANES : (tile + 1) * LANES] for j in range(members)]
            for q in range(per_tile):
                acc = None
                for j in range(members):
                    shift = ((j - q) * part) % LANES
                    moved = pltpu.roll(blocks[j], shift, 1) if shift else blocks[j]
                    acc = moved if acc is None else jnp.where(lane == j, moved, acc)
                out_ref[tile * per_tile + q, which * gates : (which + 1) * gates, :] = acc.astype(
                    BF16
                )


def taper_kernel(brick_ref, taper_ref, tiles_ref, out_ref, rows_ref, slots_ref, count_ref):
    soundings, length = taper_ref.shape
    bricks = out_ref.shape[0]
    pieces = length // LANES
    rows_ref[...] = jnp.zeros_like(rows_ref)
    slots_ref[...] = jnp.zeros_like(slots_ref)
    for f in range(pieces):
        rows_ref[pl.ds(f, soundings, stride=8), :] = taper_ref[
            :, f * LANES : (f + 1) * LANES
        ].astype(F32)
    numbers = jnp.concatenate(
        [tiles_ref[...].astype(F32), jnp.zeros((LANES - pieces, soundings), F32)], axis=0
    )
    rows_ref[pl.ds(pieces, soundings, stride=8), :] = numbers.T
    capacity = slots_ref.shape[0] // bricks
    clear_counts(count_ref)

    def place(s, _):
        slot = slot_of(brick_ref, count_ref, s, capacity)
        slots_ref[slot] = rows_ref[pl.ds(pl.multiple_of(s * 8, 8), 8), :]
        return 0

    lax.fori_loop(0, soundings, place, 0)
    out_ref[...] = slots_ref[...].reshape(bricks, 8 * capacity, LANES).astype(BF16)


def owner_kernel(
    brick_ref, got_ref, observed_ref, noise_ref, taper_ref, send_ref, wide_ref, turned_ref, count_ref
):
    sources = got_ref.shape[0]
    soundings, gates = observed_ref.shape
    seen_all = observed_ref[...].T
    noise_all = noise_ref[...].T
    rows = 2 * gates
    per_lane = LANES // soundings
    bricks = count_ref.shape[0]
    mems = send_ref.shape[0] // bricks
    block = LANES // mems
    capacity = taper_ref.shape[1] // 8
    filled = capacity * block
    scale = 1.0 / (LANES - 1.0)
    send_ref[:, :filled, :] = jnp.zeros((mems * bricks, filled, LANES), BF16)
    for m in range(mems):
        send_ref[m * bricks : (m + 1) * bricks, filled:, :] = taper_ref[...]
    clear_counts(count_ref)
    wide_ref[...] = got_ref[...].reshape(sources * rows, LANES).astype(F32)
    depth = per_lane * LANES
    r = lax.broadcasted_iota(jnp.int32, (depth, depth), 0)
    c = lax.broadcasted_iota(jnp.int32, (depth, depth), 1)
    want = (c // LANES) * sources + ((c % LANES) // per_lane) + (c % per_lane) * LANES
    select = jnp.where(r == want, 1.0, 0.0).astype(BF16)
    lefts = []
    for group in range(rows // per_lane):
        stack = jnp.concatenate(
            [
                wide_ref[pl.ds(group * per_lane + k, sources, stride=rows), :]
                for k in range(per_lane)
            ],
            axis=0,
        )
        turned = stack.T
        lefts.append(
            jnp.concatenate(
                [turned[j * soundings : (j + 1) * soundings, :] for j in range(per_lane)], axis=1
            ).astype(BF16)
        )
    left = jnp.concatenate(lefts, axis=0)
    placed = jnp.dot(left, select, preferred_element_type=F32)
    for group in range(rows // per_lane):
        for k in range(per_lane):
            g = group * per_lane + k
            turned_ref[g // gates, pl.ds(g % gates, soundings, stride=gates), :] = placed[
                group * soundings : (group + 1) * soundings, k * LANES : (k + 1) * LANES
            ]
    many = LANES // gates
    count = -(-soundings // many)
    sub8 = lax.broadcasted_iota(jnp.int32, (8, LANES), 0)
    lane8 = lax.broadcasted_iota(jnp.int32, (8, LANES), 1)
    base8 = jnp.minimum(lane8 // gates, many - 1) * gates
    within8 = lane8 - base8
    row = lax.broadcasted_iota(jnp.int32, (gates, LANES), 0)
    lane = lax.broadcasted_iota(jnp.int32, (gates, LANES), 1)
    part = lane // gates
    full = lambda x: jnp.concatenate([x, jnp.zeros((LANES - x.shape[0], LANES), F32)], axis=0)
    anomalies, rights, mats = [], [], []
    for t in range(count):
        here = range(t * many, min(soundings, (t + 1) * many))
        span = slice(t * many * gates, t * many * gates + len(here) * gates)
        pred = turned_ref[0, span, :]
        pert = turned_ref[1, span, :]
        anomaly = full(pred - jnp.sum(pred, axis=1, keepdims=True) * (1.0 / LANES))
        noise = jnp.concatenate([noise_all[:, s : s + 1] for s in here], axis=0)
        observed = jnp.concatenate([seen_all[:, s : s + 1] for s in here], axis=0)
        rights.append(full(observed + noise * pert - pred))
        cov = lax.dot_general(
            anomaly,
            anomaly,
            (((1,), (1,)), ((), ())),
            precision=lax.Precision.HIGHEST,
            preferred_element_type=F32,
        )
        mat = jnp.zeros((gates, LANES), F32)
        for u in range(many):
            at = slice(u * gates, (u + 1) * gates)
            if u < len(here):
                variance = noise[at] * noise[at]
                mine = cov[at] * scale + jnp.where(row + u * gates == lane, variance, 0.0)
            else:
                mine = jnp.where(row + u * gates == lane, 1.0, 0.0)
            mat = jnp.where(part == u, mine, mat)
        anomalies.append(anomaly)
        mats.append([mat[8 * i : 8 * i + 8] for i in range(gates // 8)])
    for k in range(gates):
        index = base8 + k
        at_k = within8 == k
        home, line = divmod(k, 8)
        for t in range(count):
            tiles = mats[t]
            sides = [jnp.take_along_axis(x, index, axis=1) for x in tiles]
            top = jnp.where(at_k, 1.0, tiles[home])[line : line + 1] / sides[home][line : line + 1]
            top = jnp.broadcast_to(top, (8, LANES))
            mats[t] = [
                jnp.where(at_k, 0.0, x) - side * top if i != home
                else jnp.where(sub8 == line, top, jnp.where(at_k, 0.0, x) - side * top)
                for i, (x, side) in enumerate(zip(tiles, sides))
            ]
    for t in range(count):
        here = range(t * many, min(soundings, (t + 1) * many))
        inverse = jnp.concatenate(mats[t], axis=0)
        spread = full(
            jnp.concatenate([jnp.where(part == u, inverse, 0.0) for u in range(many)], axis=0)
        )
        solved = (
            jnp.dot(
                spread, rights[t], precision=lax.Precision.HIGHEST, preferred_element_type=F32
            )
            * scale
        )
        gain = solved.T.astype(BF16)
        rounded = anomalies[t].astype(BF16)
        which = lax.broadcasted_iota(jnp.int32, (LANES, LANES), 0) // gates
        right = jnp.concatenate(
            [jnp.where(which == u, rounded, jnp.zeros_like(rounded)) for u in range(len(here))], axis=1
        )
        weight = jnp.dot(gain, right, preferred_element_type=F32).astype(BF16)
        for u, s in enumerate(here):
            slot = slot_of(brick_ref, count_ref, s, capacity)
            first = pl.multiple_of((slot % capacity) * block, block)
            for m in range(mems):
                send_ref[m * bricks + slot // capacity, pl.ds(first, block), :] = weight[
                    m * block : (m + 1) * block, u * LANES : (u + 1) * LANES
                ]


def update_kernel(me_ref, *refs, unit, capacity, pieces):
    parts = refs[:-9]
    recv_ref, members_ref, out_ref, model_ref, taper_ref, turn_ref, tiles_ref, sems, last = refs[-9:]
    ensemble = model_ref.shape[0]
    block = members_ref.shape[0]
    mems = ensemble // block
    half = block // 2
    sources = recv_ref.shape[0]
    filled = capacity * block
    me = me_ref[0]
    spots = [(0, 0, block), (1, 0, block), (3, 0, block), (2, 0, half), (2, half, half)]
    copies = [pltpu.make_async_copy(members_ref, out_ref, sems.at[len(spots)])]
    for n, (ref, (r, start, size)) in enumerate(zip(parts, spots)):
        first = pl.multiple_of(((me - r) & (mems - 1)) * block + start, half)
        copies.append(pltpu.make_async_copy(ref, model_ref.at[pl.ds(first, size), :], sems.at[n]))
    for copy in copies:
        copy.start()
    taper_ref[...] = recv_ref[:, filled:, :].astype(F32).reshape(sources * 8 * capacity, LANES)
    for c in range(capacity):
        numbers = taper_ref[pl.ds(8 * c + pieces, sources, stride=8 * capacity), :].T
        turn_ref[c] = numbers[:8, :].astype(jnp.int32)
    table = pltpu.make_async_copy(turn_ref, tiles_ref, last)
    table.start()
    table.wait()
    for copy in copies:
        copy.wait()

    def turn(i, _):
        items = []
        for u in range(unit):
            src = i * unit + u
            for c in range(capacity):
                where = [
                    pl.multiple_of(tiles_ref[c, f, src] * LANES, LANES) for f in range(pieces)
                ]
                items.append((src, c, where))
        rises = []
        for src, c, where in items:
            cells = jnp.concatenate([model_ref[:, pl.ds(at, LANES)] for at in where], axis=1)
            weight = recv_ref[src, c * block : (c + 1) * block, :]
            rises.append(jnp.dot(weight, cells, preferred_element_type=F32))
        for (src, c, where), rise in zip(items, rises):
            rows = pl.multiple_of((src * capacity + c) * 8, 8)
            taper = taper_ref[pl.ds(rows, 8), :]
            for f in range(pieces):
                at = pl.ds(where[f], LANES)
                out_ref[:, at] = (
                    out_ref[:, at] + rise[:, f * LANES : (f + 1) * LANES] * taper[f : f + 1, :]
                )
        return 0

    lax.fori_loop(0, sources // unit, turn, 0)


def params():
    return pltpu.CompilerParams(vmem_limit_bytes=VMEM_LIMIT)


def cost(us):
    return pl.CostEstimate(flops=us * 1000000000, transcendentals=0, bytes_accessed=us * 3000000)


def vmem(n):
    return [pl.BlockSpec(memory_space=pltpu.VMEM)] * n


def smem():
    return pl.BlockSpec(memory_space=pltpu.SMEM)


def body(
    members, predicted, perturbation, observed, noise_std, taper_weights, foot_brick, foot_tiles
):
    mems = lax.axis_size("mem")
    bricks = lax.axis_size("brick")
    devices = mems * bricks
    gates = predicted.shape[1]
    soundings = observed.shape[1]
    ensemble = predicted.shape[0] * bricks
    capacity = 2
    slots = bricks * capacity
    pieces = foot_tiles.shape[1]
    brick = foot_brick[:, 0]
    sds = jax.ShapeDtypeStruct

    def shifted(x, by):
        return lax.ppermute(x, "mem", [(i, (i + by) % mems) for i in range(mems)])

    packed = pl.pallas_call(
        lambda *refs: pack_kernel(*refs, part=soundings),
        out_shape=sds((bricks, 2 * gates, LANES), BF16),
        in_specs=vmem(2),
        out_specs=vmem(1)[0],
        compiler_params=params(),
        cost_estimate=cost(3),
        name="pack",
    )(predicted, perturbation)
    got = lax.all_to_all(packed, "brick", split_axis=0, concat_axis=0, tiled=True)

    held, _ = lax.optimization_barrier((members, packed))
    model0 = held.astype(BF16)
    model1, model3 = shifted(model0, 1), shifted(model0, -1)

    brick, _ = lax.optimization_barrier((brick, packed))
    taper_rows = pl.pallas_call(
        taper_kernel,
        out_shape=sds((bricks, 8 * capacity, LANES), BF16),
        in_specs=[smem()] + vmem(2),
        out_specs=vmem(1)[0],
        scratch_shapes=[
            pltpu.VMEM((soundings * 8, LANES), F32),
            pltpu.VMEM((slots, 8, LANES), F32),
            pltpu.SMEM((bricks,), jnp.int32),
        ],
        compiler_params=params(),
        cost_estimate=cost(2),
        name="route_taper",
    )(brick, taper_weights, foot_tiles.T)

    weight_send = pl.pallas_call(
        owner_kernel,
        out_shape=sds((devices, capacity * (ensemble // mems + 8), ensemble), BF16),
        in_specs=[smem()] + vmem(4),
        out_specs=vmem(1)[0],
        scratch_shapes=[
            pltpu.VMEM((bricks * 2 * gates, LANES), F32),
            pltpu.VMEM((2, soundings * gates, LANES), F32),
            pltpu.SMEM((bricks,), jnp.int32),
        ],
        compiler_params=params(),
        cost_estimate=cost(15),
        name="owner",
    )(brick, got, observed.T, noise_std.T, taper_rows)
    weight_send, model1, model3 = lax.optimization_barrier((weight_send, model1, model3))
    half = members.shape[0] // 2
    upper2, lower2 = shifted(model1[:half], 1), shifted(model3[half:], -1)
    blocks = (model0, model1, model3, upper2, lower2)
    weight_recv = lax.all_to_all(
        weight_send, ("mem", "brick"), split_axis=0, concat_axis=0, tiled=True
    )
    me = lax.axis_index("mem").astype(jnp.int32).reshape(1)
    hbm = pl.BlockSpec(memory_space=pl.ANY)
    weight_recv = pltpu.with_memory_space_constraint(weight_recv, pltpu.VMEM)
    return pl.pallas_call(
        lambda *refs: update_kernel(*refs, unit=16, capacity=capacity, pieces=pieces),
        out_shape=sds(members.shape, F32),
        in_specs=[smem()] + [hbm] * len(blocks) + vmem(1) + [hbm],
        out_specs=vmem(1)[0],
        scratch_shapes=[
            pltpu.VMEM((ensemble, members.shape[1]), BF16),
            pltpu.VMEM((devices * 8 * capacity, LANES), F32),
            pltpu.VMEM((capacity, 8, devices), jnp.int32),
            pltpu.SMEM((capacity, 8, devices), jnp.int32),
            pltpu.SemaphoreType.DMA((len(blocks) + 1,)),
            pltpu.SemaphoreType.DMA(()),
        ],
        compiler_params=params(),
        cost_estimate=cost(20),
        name="update",
    )(me, *blocks, weight_recv, members)


def solution(mesh):
    in_specs = (
        P("mem", "brick"),
        P("brick", None, "mem"),
        P("brick", None, "mem"),
        P(None, ("mem", "brick")),
        P(None, ("mem", "brick")),
        P(("mem", "brick"), None),
        P(("mem", "brick"), None),
        P(("mem", "brick"), None),
    )
    out_specs = P("mem", "brick")
    return jax.shard_map(body, mesh=mesh, in_specs=in_specs, out_specs=out_specs, check_vma=False)
```

```python
import jax
import jax.numpy as jnp
from jax import lax
from jax.experimental import pallas as pl
from jax.experimental.pallas import tpu as pltpu
from jax.sharding import PartitionSpec as P

F32 = jnp.float32
BF16 = jnp.bfloat16
VMEM_LIMIT = 56 * 1024 * 1024
LANES = 128


def slot_of(brick_ref, count_ref, s, capacity):
    dest = brick_ref[s]
    rank = jnp.minimum(count_ref[dest], capacity - 1)
    count_ref[dest] = rank + 1
    return dest * capacity + rank


def clear_counts(count_ref):
    def clear(i, _):
        count_ref[i] = 0
        return 0

    lax.fori_loop(0, count_ref.shape[0], clear, 0)


def pack_kernel(pred_ref, pert_ref, out_ref, *, part):
    members, gates, width = pred_ref.shape
    per_tile = LANES // part
    lane = lax.broadcasted_iota(jnp.int32, (gates, LANES), 1) // part
    for which, ref in enumerate((pred_ref, pert_ref)):
        for tile in range(width // LANES):
            blocks = [ref[j, :, tile * LANES : (tile + 1) * LANES] for j in range(members)]
            for q in range(per_tile):
                acc = None
                for j in range(members):
                    shift = ((j - q) * part) % LANES
                    moved = pltpu.roll(blocks[j], shift, 1) if shift else blocks[j]
                    acc = moved if acc is None else jnp.where(lane == j, moved, acc)
                out_ref[tile * per_tile + q, which * gates : (which + 1) * gates, :] = acc.astype(
                    BF16
                )


def taper_kernel(brick_ref, taper_ref, tiles_ref, out_ref, rows_ref, slots_ref, count_ref):
    soundings, length = taper_ref.shape
    bricks = out_ref.shape[0]
    pieces = length // LANES
    rows_ref[...] = jnp.zeros_like(rows_ref)
    slots_ref[...] = jnp.zeros_like(slots_ref)
    for f in range(pieces):
        rows_ref[pl.ds(f, soundings, stride=8), :] = taper_ref[
            :, f * LANES : (f + 1) * LANES
        ].astype(F32)
    numbers = jnp.concatenate(
        [tiles_ref[...].astype(F32), jnp.zeros((LANES - pieces, soundings), F32)], axis=0
    )
    rows_ref[pl.ds(pieces, soundings, stride=8), :] = numbers.T
    capacity = slots_ref.shape[0] // bricks
    clear_counts(count_ref)

    def place(s, _):
        slot = slot_of(brick_ref, count_ref, s, capacity)
        slots_ref[slot] = rows_ref[pl.ds(pl.multiple_of(s * 8, 8), 8), :]
        return 0

    lax.fori_loop(0, soundings, place, 0)
    out_ref[...] = slots_ref[...].reshape(bricks, 8 * capacity, LANES).astype(BF16)


def owner_kernel(
    brick_ref, got_ref, observed_ref, noise_ref, taper_ref, send_ref, wide_ref, turned_ref, count_ref
):
    sources = got_ref.shape[0]
    soundings, gates = observed_ref.shape
    seen_all = observed_ref[...].T
    noise_all = noise_ref[...].T
    rows = 2 * gates
    per_lane = LANES // soundings
    bricks = count_ref.shape[0]
    mems = send_ref.shape[0] // bricks
    block = LANES // mems
    capacity = taper_ref.shape[1] // 8
    filled = capacity * block
    scale = 1.0 / (LANES - 1.0)
    send_ref[:, :filled, :] = jnp.zeros((mems * bricks, filled, LANES), BF16)
    for m in range(mems):
        send_ref[m * bricks : (m + 1) * bricks, filled:, :] = taper_ref[...]
    clear_counts(count_ref)
    wide_ref[...] = got_ref[...].reshape(sources * rows, LANES).astype(F32)
    depth = per_lane * LANES
    r = lax.broadcasted_iota(jnp.int32, (depth, depth), 0)
    c = lax.broadcasted_iota(jnp.int32, (depth, depth), 1)
    want = (c // LANES) * sources + ((c % LANES) // per_lane) + (c % per_lane) * LANES
    select = jnp.where(r == want, 1.0, 0.0).astype(BF16)
    lefts = []
    for group in range(rows // per_lane):
        stack = jnp.concatenate(
            [
                wide_ref[pl.ds(group * per_lane + k, sources, stride=rows), :]
                for k in range(per_lane)
            ],
            axis=0,
        )
        turned = stack.astype(BF16).T
        lefts.append(
            jnp.concatenate(
                [turned[j * soundings : (j + 1) * soundings, :] for j in range(per_lane)], axis=1
            ).astype(BF16)
        )
    left = jnp.concatenate(lefts, axis=0)
    placed = jnp.dot(left, select, preferred_element_type=F32)
    for group in range(rows // per_lane):
        for k in range(per_lane):
            g = group * per_lane + k
            turned_ref[g // gates, pl.ds(g % gates, soundings, stride=gates), :] = placed[
                group * soundings : (group + 1) * soundings, k * LANES : (k + 1) * LANES
            ]
    many = LANES // gates
    count = -(-soundings // many)
    sub8 = lax.broadcasted_iota(jnp.int32, (8, LANES), 0)
    lane8 = lax.broadcasted_iota(jnp.int32, (8, LANES), 1)
    base8 = jnp.minimum(lane8 // gates, many - 1) * gates
    within8 = lane8 - base8
    row = lax.broadcasted_iota(jnp.int32, (gates, LANES), 0)
    lane = lax.broadcasted_iota(jnp.int32, (gates, LANES), 1)
    part = lane // gates
    full = lambda x: jnp.concatenate([x, jnp.zeros((LANES - x.shape[0], LANES), F32)], axis=0)
    anomalies, rights, mats = [], [], []
    for t in range(count):
        here = range(t * many, min(soundings, (t + 1) * many))
        span = slice(t * many * gates, t * many * gates + len(here) * gates)
        pred = turned_ref[0, span, :]
        pert = turned_ref[1, span, :]
        anomaly = full(pred - jnp.sum(pred, axis=1, keepdims=True) * (1.0 / LANES))
        noise = jnp.concatenate([noise_all[:, s : s + 1] for s in here], axis=0)
        observed = jnp.concatenate([seen_all[:, s : s + 1] for s in here], axis=0)
        rights.append(full(observed + noise * pert - pred))
        cov = lax.dot_general(
            anomaly,
            anomaly,
            (((1,), (1,)), ((), ())),
            precision=lax.Precision.HIGHEST,
            preferred_element_type=F32,
        )
        mat = jnp.zeros((gates, LANES), F32)
        for u in range(many):
            at = slice(u * gates, (u + 1) * gates)
            if u < len(here):
                variance = noise[at] * noise[at]
                mine = cov[at] * scale + jnp.where(row + u * gates == lane, variance, 0.0)
            else:
                mine = jnp.where(row + u * gates == lane, 1.0, 0.0)
            mat = jnp.where(part == u, mine, mat)
        anomalies.append(anomaly)
        mats.append([mat[8 * i : 8 * i + 8] for i in range(gates // 8)])
    for k in range(gates):
        index = base8 + k
        at_k = within8 == k
        home, line = divmod(k, 8)
        for t in range(count):
            tiles = mats[t]
            sides = [jnp.take_along_axis(x, index, axis=1) for x in tiles]
            top = jnp.where(at_k, 1.0, tiles[home])[line : line + 1] / sides[home][line : line + 1]
            top = jnp.broadcast_to(top, (8, LANES))
            mats[t] = [
                jnp.where(at_k, 0.0, x) - side * top if i != home
                else jnp.where(sub8 == line, top, jnp.where(at_k, 0.0, x) - side * top)
                for i, (x, side) in enumerate(zip(tiles, sides))
            ]
    for t in range(count):
        here = range(t * many, min(soundings, (t + 1) * many))
        inverse = jnp.concatenate(mats[t], axis=0)
        spread = full(
            jnp.concatenate([jnp.where(part == u, inverse, 0.0) for u in range(many)], axis=0)
        )
        solved = (
            jnp.dot(
                spread, rights[t], precision=lax.Precision.HIGHEST, preferred_element_type=F32
            )
            * scale
        )
        gain = solved.astype(BF16).T
        rounded = anomalies[t].astype(BF16)
        which = lax.broadcasted_iota(jnp.int32, (LANES, LANES), 0) // gates
        right = jnp.concatenate(
            [jnp.where(which == u, rounded, jnp.zeros_like(rounded)) for u in range(len(here))], axis=1
        )
        weight = jnp.dot(gain, right, preferred_element_type=F32).astype(BF16)
        for u, s in enumerate(here):
            slot = slot_of(brick_ref, count_ref, s, capacity)
            first = pl.multiple_of((slot % capacity) * block, block)
            for m in range(mems):
                send_ref[m * bricks + slot // capacity, pl.ds(first, block), :] = weight[
                    m * block : (m + 1) * block, u * LANES : (u + 1) * LANES
                ]


def assemble_kernel(me_ref, *refs):
    parts = refs[:-2]
    out_ref, sems = refs[-2:]
    half = parts[0].shape[0]
    mems = len(parts) // 2
    me = me_ref[0]
    copies = []
    for n, ref in enumerate(parts):
        first = ((me - n // 2) & (mems - 1)) * 2 * half + (n % 2) * half
        first = pl.multiple_of(first, half)
        copies.append(pltpu.make_async_copy(ref, out_ref.at[pl.ds(first, half), :], sems.at[n]))
    for copy in copies:
        copy.start()
    for copy in copies:
        copy.wait()


def update_kernel(
    model_hbm_ref,
    recv_ref,
    members_ref,
    out_ref,
    model_ref,
    taper_ref,
    turn_ref,
    tiles_ref,
    model_sem,
    held_sem,
    table_sem,
    *,
    unit,
    capacity,
    pieces,
):
    sources = recv_ref.shape[0]
    block = members_ref.shape[0]
    filled = capacity * block
    model = pltpu.make_async_copy(model_hbm_ref, model_ref, model_sem)
    held = pltpu.make_async_copy(members_ref, out_ref, held_sem)
    model.start()
    held.start()
    taper_ref[...] = recv_ref[:, filled:, :].astype(F32).reshape(sources * 8 * capacity, LANES)
    for c in range(capacity):
        numbers = taper_ref[pl.ds(8 * c + pieces, sources, stride=8 * capacity), :].T
        turn_ref[c] = numbers[:8, :].astype(jnp.int32)
    table = pltpu.make_async_copy(turn_ref, tiles_ref, table_sem)
    table.start()
    table.wait()
    model.wait()
    held.wait()

    def turn(i, _):
        items = []
        for u in range(unit):
            src = i * unit + u
            for c in range(capacity):
                where = [
                    pl.multiple_of(tiles_ref[c, f, src] * LANES, LANES) for f in range(pieces)
                ]
                items.append((src, c, where))
        rises = []
        for src, c, where in items:
            cells = jnp.concatenate([model_ref[:, pl.ds(at, LANES)] for at in where], axis=1)
            weight = recv_ref[src, c * block : (c + 1) * block, :]
            rises.append(jnp.dot(weight, cells, preferred_element_type=F32))
        for (src, c, where), rise in zip(items, rises):
            rows = pl.multiple_of((src * capacity + c) * 8, 8)
            taper = taper_ref[pl.ds(rows, 8), :]
            for f in range(pieces):
                at = pl.ds(where[f], LANES)
                out_ref[:, at] = (
                    out_ref[:, at] + rise[:, f * LANES : (f + 1) * LANES] * taper[f : f + 1, :]
                )
        return 0

    lax.fori_loop(0, sources // unit, turn, 0)


def params():
    return pltpu.CompilerParams(vmem_limit_bytes=VMEM_LIMIT)


def cost(us):
    return pl.CostEstimate(flops=us * 1000000000, transcendentals=0, bytes_accessed=us * 3000000)


def vmem(n):
    return [pl.BlockSpec(memory_space=pltpu.VMEM)] * n


def smem():
    return pl.BlockSpec(memory_space=pltpu.SMEM)


def body(
    members, predicted, perturbation, observed, noise_std, taper_weights, foot_brick, foot_tiles
):
    mems = lax.axis_size("mem")
    bricks = lax.axis_size("brick")
    devices = mems * bricks
    gates = predicted.shape[1]
    soundings = observed.shape[1]
    ensemble = predicted.shape[0] * bricks
    capacity = 2
    slots = bricks * capacity
    pieces = foot_tiles.shape[1]
    brick = foot_brick[:, 0]
    sds = jax.ShapeDtypeStruct

    def shifted(x, by):
        return lax.ppermute(x, "mem", [(i, (i + by) % mems) for i in range(mems)])

    packed = pl.pallas_call(
        lambda *refs: pack_kernel(*refs, part=soundings),
        out_shape=sds((bricks, 2 * gates, LANES), BF16),
        in_specs=vmem(2),
        out_specs=vmem(1)[0],
        compiler_params=params(),
        cost_estimate=cost(3),
        name="pack",
    )(predicted, perturbation)
    got = lax.all_to_all(packed, "brick", split_axis=0, concat_axis=0, tiled=True)

    held, _ = lax.optimization_barrier((members, packed))
    half = members.shape[0] // 2
    upper, lower = held[:half].astype(BF16), held[half:].astype(BF16)
    upper1, lower3 = shifted(upper, 1), shifted(lower, -1)
    lower1, upper3 = shifted(lower, 1), shifted(upper, -1)

    brick, _ = lax.optimization_barrier((brick, packed))
    taper_rows = pl.pallas_call(
        taper_kernel,
        out_shape=sds((bricks, 8 * capacity, LANES), BF16),
        in_specs=[smem()] + vmem(2),
        out_specs=vmem(1)[0],
        scratch_shapes=[
            pltpu.VMEM((soundings * 8, LANES), F32),
            pltpu.VMEM((slots, 8, LANES), F32),
            pltpu.SMEM((bricks,), jnp.int32),
        ],
        compiler_params=params(),
        cost_estimate=cost(2),
        name="route_taper",
    )(brick, taper_weights, foot_tiles.T)

    weight_send = pl.pallas_call(
        owner_kernel,
        out_shape=sds((devices, capacity * (ensemble // mems + 8), ensemble), BF16),
        in_specs=[smem()] + vmem(4),
        out_specs=vmem(1)[0],
        scratch_shapes=[
            pltpu.VMEM((bricks * 2 * gates, LANES), F32),
            pltpu.VMEM((2, soundings * gates, LANES), F32),
            pltpu.SMEM((bricks,), jnp.int32),
        ],
        compiler_params=params(),
        cost_estimate=cost(15),
        name="owner",
    )(brick, got, observed.T, noise_std.T, taper_rows)
    weight_send, upper1, lower1, upper3, lower3 = lax.optimization_barrier(
        (weight_send, upper1, lower1, upper3, lower3)
    )
    upper2, lower2 = shifted(upper1, 1), shifted(lower3, -1)
    halves = (upper, lower, upper1, lower1, upper2, lower2, upper3, lower3)
    weight_recv = lax.all_to_all(
        weight_send, ("mem", "brick"), split_axis=0, concat_axis=0, tiled=True
    )
    me = lax.axis_index("mem").astype(jnp.int32).reshape(1)
    hbm = pl.BlockSpec(memory_space=pl.ANY)
    model_all = pl.pallas_call(
        assemble_kernel,
        out_shape=sds((ensemble, members.shape[1]), BF16),
        in_specs=[smem()] + [hbm] * (2 * mems),
        out_specs=vmem(1)[0],
        scratch_shapes=[pltpu.SemaphoreType.DMA((2 * mems,))],
        compiler_params=params(),
        cost_estimate=cost(40),
        name="assemble",
    )(me, *halves)
    weight_recv = pltpu.with_memory_space_constraint(weight_recv, pltpu.VMEM)
    return pl.pallas_call(
        lambda *refs: update_kernel(*refs, unit=16, capacity=capacity, pieces=pieces),
        out_shape=sds(members.shape, F32),
        in_specs=[hbm] + vmem(1) + [hbm],
        out_specs=vmem(1)[0],
        scratch_shapes=[
            pltpu.VMEM(model_all.shape, BF16),
            pltpu.VMEM((devices * 8 * capacity, LANES), F32),
            pltpu.VMEM((capacity, 8, devices), jnp.int32),
            pltpu.SMEM((capacity, 8, devices), jnp.int32),
            pltpu.SemaphoreType.DMA(()),
            pltpu.SemaphoreType.DMA(()),
            pltpu.SemaphoreType.DMA(()),
        ],
        compiler_params=params(),
        cost_estimate=cost(20),
        name="update",
    )(model_all, weight_recv, members)


def solution(mesh):
    in_specs = (
        P("mem", "brick"),
        P("brick", None, "mem"),
        P("brick", None, "mem"),
        P(None, ("mem", "brick")),
        P(None, ("mem", "brick")),
        P(("mem", "brick"), None),
        P(("mem", "brick"), None),
        P(("mem", "brick"), None),
    )
    out_specs = P("mem", "brick")
    return jax.shard_map(body, mesh=mesh, in_specs=in_specs, out_specs=out_specs, check_vma=False)
```

```python
import jax
import jax.numpy as jnp
from jax import lax
from jax.experimental import pallas as pl
from jax.experimental.pallas import tpu as pltpu
from jax.sharding import PartitionSpec as P

F32 = jnp.float32
BF16 = jnp.bfloat16
VMEM_LIMIT = 56 * 1024 * 1024
LANES = 128


def slot_of(brick_ref, count_ref, s, capacity):
    dest = brick_ref[s]
    rank = jnp.minimum(count_ref[dest], capacity - 1)
    count_ref[dest] = rank + 1
    return dest * capacity + rank


def clear_counts(count_ref):
    def clear(i, _):
        count_ref[i] = 0
        return 0

    lax.fori_loop(0, count_ref.shape[0], clear, 0)


def pack_kernel(pred_ref, pert_ref, out_ref, *, part):
    members, gates, width = pred_ref.shape
    per_tile = LANES // part
    lane = lax.broadcasted_iota(jnp.int32, (gates, LANES), 1) // part
    for which, ref in enumerate((pred_ref, pert_ref)):
        for tile in range(width // LANES):
            blocks = [ref[j, :, tile * LANES : (tile + 1) * LANES] for j in range(members)]
            for q in range(per_tile):
                acc = None
                for j in range(members):
                    shift = ((j - q) * part) % LANES
                    moved = pltpu.roll(blocks[j], shift, 1) if shift else blocks[j]
                    acc = moved if acc is None else jnp.where(lane == j, moved, acc)
                out_ref[tile * per_tile + q, which * gates : (which + 1) * gates, :] = acc.astype(
                    BF16
                )


def taper_kernel(brick_ref, taper_ref, tiles_ref, out_ref, rows_ref, slots_ref, count_ref):
    soundings, length = taper_ref.shape
    bricks = out_ref.shape[0]
    pieces = length // LANES
    rows_ref[...] = jnp.zeros_like(rows_ref)
    slots_ref[...] = jnp.zeros_like(slots_ref)
    for f in range(pieces):
        rows_ref[pl.ds(f, soundings, stride=8), :] = taper_ref[
            :, f * LANES : (f + 1) * LANES
        ].astype(F32)
    numbers = jnp.concatenate(
        [tiles_ref[...].astype(F32), jnp.zeros((LANES - pieces, soundings), F32)], axis=0
    )
    rows_ref[pl.ds(pieces, soundings, stride=8), :] = numbers.T
    capacity = slots_ref.shape[0] // bricks
    clear_counts(count_ref)

    def place(s, _):
        slot = slot_of(brick_ref, count_ref, s, capacity)
        slots_ref[slot] = rows_ref[pl.ds(pl.multiple_of(s * 8, 8), 8), :]
        return 0

    lax.fori_loop(0, soundings, place, 0)
    out_ref[...] = slots_ref[...].reshape(bricks, 8 * capacity, LANES).astype(BF16)


def owner_kernel(
    brick_ref, got_ref, observed_ref, noise_ref, taper_ref, send_ref, wide_ref, turned_ref, count_ref
):
    sources = got_ref.shape[0]
    soundings, gates = observed_ref.shape
    seen_all = observed_ref[...].T
    noise_all = noise_ref[...].T
    rows = 2 * gates
    per_lane = LANES // soundings
    bricks = count_ref.shape[0]
    mems = send_ref.shape[0] // bricks
    block = LANES // mems
    capacity = taper_ref.shape[1] // 8
    filled = capacity * block
    scale = 1.0 / (LANES - 1.0)
    send_ref[:, :filled, :] = jnp.zeros((mems * bricks, filled, LANES), BF16)
    for m in range(mems):
        send_ref[m * bricks : (m + 1) * bricks, filled:, :] = taper_ref[...]
    clear_counts(count_ref)
    wide_ref[...] = got_ref[...].reshape(sources * rows, LANES).astype(F32)
    depth = per_lane * LANES
    r = lax.broadcasted_iota(jnp.int32, (depth, depth), 0)
    c = lax.broadcasted_iota(jnp.int32, (depth, depth), 1)
    want = (c // LANES) * sources + ((c % LANES) // per_lane) + (c % per_lane) * LANES
    select = jnp.where(r == want, 1.0, 0.0).astype(BF16)
    lefts = []
    for group in range(rows // per_lane):
        stack = jnp.concatenate(
            [
                wide_ref[pl.ds(group * per_lane + k, sources, stride=rows), :]
                for k in range(per_lane)
            ],
            axis=0,
        )
        turned = stack.astype(BF16).T
        lefts.append(
            jnp.concatenate(
                [turned[j * soundings : (j + 1) * soundings, :] for j in range(per_lane)], axis=1
            ).astype(BF16)
        )
    left = jnp.concatenate(lefts, axis=0)
    placed = jnp.dot(left, select, preferred_element_type=F32)
    for group in range(rows // per_lane):
        for k in range(per_lane):
            g = group * per_lane + k
            turned_ref[g // gates, pl.ds(g % gates, soundings, stride=gates), :] = placed[
                group * soundings : (group + 1) * soundings, k * LANES : (k + 1) * LANES
            ]
    many = LANES // gates
    count = -(-soundings // many)
    sub8 = lax.broadcasted_iota(jnp.int32, (8, LANES), 0)
    lane8 = lax.broadcasted_iota(jnp.int32, (8, LANES), 1)
    base8 = jnp.minimum(lane8 // gates, many - 1) * gates
    within8 = lane8 - base8
    row = lax.broadcasted_iota(jnp.int32, (gates, LANES), 0)
    lane = lax.broadcasted_iota(jnp.int32, (gates, LANES), 1)
    part = lane // gates
    full = lambda x: jnp.concatenate([x, jnp.zeros((LANES - x.shape[0], LANES), F32)], axis=0)
    anomalies, rights, mats = [], [], []
    for t in range(count):
        here = range(t * many, min(soundings, (t + 1) * many))
        span = slice(t * many * gates, t * many * gates + len(here) * gates)
        pred = turned_ref[0, span, :]
        pert = turned_ref[1, span, :]
        anomaly = full(pred - jnp.sum(pred, axis=1, keepdims=True) * (1.0 / LANES))
        noise = jnp.concatenate([noise_all[:, s : s + 1] for s in here], axis=0)
        observed = jnp.concatenate([seen_all[:, s : s + 1] for s in here], axis=0)
        rights.append(full(observed + noise * pert - pred))
        cov = lax.dot_general(
            anomaly,
            anomaly,
            (((1,), (1,)), ((), ())),
            precision=lax.Precision.HIGHEST,
            preferred_element_type=F32,
        )
        mat = jnp.zeros((gates, LANES), F32)
        for u in range(many):
            at = slice(u * gates, (u + 1) * gates)
            if u < len(here):
                variance = noise[at] * noise[at]
                mine = cov[at] * scale + jnp.where(row + u * gates == lane, variance, 0.0)
            else:
                mine = jnp.where(row + u * gates == lane, 1.0, 0.0)
            mat = jnp.where(part == u, mine, mat)
        anomalies.append(anomaly)
        mats.append([mat[8 * i : 8 * i + 8] for i in range(gates // 8)])
    for k in range(gates):
        index = base8 + k
        at_k = within8 == k
        home, line = divmod(k, 8)
        for t in range(count):
            tiles = mats[t]
            sides = [jnp.take_along_axis(x, index, axis=1) for x in tiles]
            top = jnp.where(at_k, 1.0, tiles[home])[line : line + 1] / sides[home][line : line + 1]
            top = jnp.broadcast_to(top, (8, LANES))
            mats[t] = [
                jnp.where(at_k, 0.0, x) - side * top if i != home
                else jnp.where(sub8 == line, top, jnp.where(at_k, 0.0, x) - side * top)
                for i, (x, side) in enumerate(zip(tiles, sides))
            ]
    for t in range(count):
        here = range(t * many, min(soundings, (t + 1) * many))
        inverse = jnp.concatenate(mats[t], axis=0)
        spread = full(
            jnp.concatenate([jnp.where(part == u, inverse, 0.0) for u in range(many)], axis=0)
        )
        solved = (
            jnp.dot(
                spread, rights[t], precision=lax.Precision.HIGHEST, preferred_element_type=F32
            )
            * scale
        )
        gain = solved.astype(BF16).T
        rounded = anomalies[t].astype(BF16)
        which = lax.broadcasted_iota(jnp.int32, (LANES, LANES), 0) // gates
        right = jnp.concatenate(
            [jnp.where(which == u, rounded, jnp.zeros_like(rounded)) for u in range(len(here))], axis=1
        )
        weight = jnp.dot(gain, right, preferred_element_type=F32).astype(BF16)
        for u, s in enumerate(here):
            slot = slot_of(brick_ref, count_ref, s, capacity)
            first = pl.multiple_of((slot % capacity) * block, block)
            for m in range(mems):
                send_ref[m * bricks + slot // capacity, pl.ds(first, block), :] = weight[
                    m * block : (m + 1) * block, u * LANES : (u + 1) * LANES
                ]


def assemble_kernel(me_ref, *refs):
    parts = refs[:-2]
    out_ref, sems = refs[-2:]
    half = parts[0].shape[0]
    mems = len(parts) // 2
    me = me_ref[0]
    copies = []
    for n, ref in enumerate(parts):
        first = ((me - n // 2) & (mems - 1)) * 2 * half + (n % 2) * half
        first = pl.multiple_of(first, half)
        copies.append(pltpu.make_async_copy(ref, out_ref.at[pl.ds(first, half), :], sems.at[n]))
    for copy in copies:
        copy.start()
    for copy in copies:
        copy.wait()


def update_kernel(
    model_hbm_ref,
    recv_ref,
    members_ref,
    out_ref,
    model_ref,
    taper_ref,
    turn_ref,
    tiles_ref,
    model_sem,
    held_sem,
    table_sem,
    *,
    unit,
    capacity,
    pieces,
):
    sources = recv_ref.shape[0]
    block = members_ref.shape[0]
    filled = capacity * block
    model = pltpu.make_async_copy(model_hbm_ref, model_ref, model_sem)
    held = pltpu.make_async_copy(members_ref, out_ref, held_sem)
    model.start()
    held.start()
    taper_ref[...] = recv_ref[:, filled:, :].astype(F32).reshape(sources * 8 * capacity, LANES)
    for c in range(capacity):
        numbers = taper_ref[pl.ds(8 * c + pieces, sources, stride=8 * capacity), :].T
        turn_ref[c] = numbers[:8, :].astype(jnp.int32)
    table = pltpu.make_async_copy(turn_ref, tiles_ref, table_sem)
    table.start()
    table.wait()
    model.wait()
    held.wait()

    def turn(i, _):
        items = []
        for u in range(unit):
            src = i * unit + u
            for c in range(capacity):
                where = [
                    pl.multiple_of(tiles_ref[c, f, src] * LANES, LANES) for f in range(pieces)
                ]
                items.append((src, c, where))
        rises = []
        for src, c, where in items:
            cells = jnp.concatenate([model_ref[:, pl.ds(at, LANES)] for at in where], axis=1)
            weight = recv_ref[src, c * block : (c + 1) * block, :]
            rises.append(jnp.dot(weight, cells, preferred_element_type=F32))
        for (src, c, where), rise in zip(items, rises):
            rows = pl.multiple_of((src * capacity + c) * 8, 8)
            taper = taper_ref[pl.ds(rows, 8), :]
            for f in range(pieces):
                at = pl.ds(where[f], LANES)
                out_ref[:, at] = (
                    out_ref[:, at] + rise[:, f * LANES : (f + 1) * LANES] * taper[f : f + 1, :]
                )
        return 0

    lax.fori_loop(0, sources // unit, turn, 0)


def params():
    return pltpu.CompilerParams(vmem_limit_bytes=VMEM_LIMIT)


def cost(us):
    return pl.CostEstimate(flops=us * 1000000000, transcendentals=0, bytes_accessed=us * 3000000)


def vmem(n):
    return [pl.BlockSpec(memory_space=pltpu.VMEM)] * n


def smem():
    return pl.BlockSpec(memory_space=pltpu.SMEM)


def body(
    members, predicted, perturbation, observed, noise_std, taper_weights, foot_brick, foot_tiles
):
    mems = lax.axis_size("mem")
    bricks = lax.axis_size("brick")
    devices = mems * bricks
    gates = predicted.shape[1]
    soundings = observed.shape[1]
    ensemble = predicted.shape[0] * bricks
    capacity = 2
    slots = bricks * capacity
    pieces = foot_tiles.shape[1]
    brick = foot_brick[:, 0]
    sds = jax.ShapeDtypeStruct

    def shifted(x, by):
        return lax.ppermute(x, "mem", [(i, (i + by) % mems) for i in range(mems)])

    packed = pl.pallas_call(
        lambda *refs: pack_kernel(*refs, part=soundings),
        out_shape=sds((bricks, 2 * gates, LANES), BF16),
        in_specs=vmem(2),
        out_specs=vmem(1)[0],
        compiler_params=params(),
        cost_estimate=cost(3),
        name="pack",
    )(predicted, perturbation)
    got = lax.all_to_all(packed, "brick", split_axis=0, concat_axis=0, tiled=True)

    held, _ = lax.optimization_barrier((members, packed))
    half = members.shape[0] // 2
    upper, lower = held[:half].astype(BF16), held[half:].astype(BF16)
    upper1, lower3 = shifted(upper, 1), shifted(lower, -1)
    lower1, upper3 = shifted(lower, 1), shifted(upper, -1)

    brick, _ = lax.optimization_barrier((brick, packed))
    taper_rows = pl.pallas_call(
        taper_kernel,
        out_shape=sds((bricks, 8 * capacity, LANES), BF16),
        in_specs=[smem()] + vmem(2),
        out_specs=vmem(1)[0],
        scratch_shapes=[
            pltpu.VMEM((soundings * 8, LANES), F32),
            pltpu.VMEM((slots, 8, LANES), F32),
            pltpu.SMEM((bricks,), jnp.int32),
        ],
        compiler_params=params(),
        cost_estimate=cost(2),
        name="route_taper",
    )(brick, taper_weights, foot_tiles.T)

    got = pltpu.with_memory_space_constraint(got, pltpu.VMEM)
    weight_send = pl.pallas_call(
        owner_kernel,
        out_shape=sds((devices, capacity * (ensemble // mems + 8), ensemble), BF16),
        in_specs=[smem()] + vmem(4),
        out_specs=vmem(1)[0],
        scratch_shapes=[
            pltpu.VMEM((bricks * 2 * gates, LANES), F32),
            pltpu.VMEM((2, soundings * gates, LANES), F32),
            pltpu.SMEM((bricks,), jnp.int32),
        ],
        compiler_params=params(),
        cost_estimate=cost(15),
        name="owner",
    )(brick, got, observed.T, noise_std.T, taper_rows)
    weight_send, upper1, lower1, upper3, lower3 = lax.optimization_barrier(
        (weight_send, upper1, lower1, upper3, lower3)
    )
    upper2, lower2 = shifted(upper1, 1), shifted(lower3, -1)
    halves = (upper, lower, upper1, lower1, upper2, lower2, upper3, lower3)
    weight_recv = lax.all_to_all(
        weight_send, ("mem", "brick"), split_axis=0, concat_axis=0, tiled=True
    )
    me = lax.axis_index("mem").astype(jnp.int32).reshape(1)
    hbm = pl.BlockSpec(memory_space=pl.ANY)
    model_all = pl.pallas_call(
        assemble_kernel,
        out_shape=sds((ensemble, members.shape[1]), BF16),
        in_specs=[smem()] + [hbm] * (2 * mems),
        out_specs=vmem(1)[0],
        scratch_shapes=[pltpu.SemaphoreType.DMA((2 * mems,))],
        compiler_params=params(),
        cost_estimate=cost(40),
        name="assemble",
    )(me, *halves)
    weight_recv = pltpu.with_memory_space_constraint(weight_recv, pltpu.VMEM)
    return pl.pallas_call(
        lambda *refs: update_kernel(*refs, unit=16, capacity=capacity, pieces=pieces),
        out_shape=sds(members.shape, F32),
        in_specs=[hbm] + vmem(1) + [hbm],
        out_specs=vmem(1)[0],
        scratch_shapes=[
            pltpu.VMEM(model_all.shape, BF16),
            pltpu.VMEM((devices * 8 * capacity, LANES), F32),
            pltpu.VMEM((capacity, 8, devices), jnp.int32),
            pltpu.SMEM((capacity, 8, devices), jnp.int32),
            pltpu.SemaphoreType.DMA(()),
            pltpu.SemaphoreType.DMA(()),
            pltpu.SemaphoreType.DMA(()),
        ],
        compiler_params=params(),
        cost_estimate=cost(20),
        name="update",
    )(model_all, weight_recv, members)


def solution(mesh):
    in_specs = (
        P("mem", "brick"),
        P("brick", None, "mem"),
        P("brick", None, "mem"),
        P(None, ("mem", "brick")),
        P(None, ("mem", "brick")),
        P(("mem", "brick"), None),
        P(("mem", "brick"), None),
        P(("mem", "brick"), None),
    )
    out_specs = P("mem", "brick")
    return jax.shard_map(body, mesh=mesh, in_specs=in_specs, out_specs=out_specs, check_vma=False)
```

```python
import jax
import jax.numpy as jnp
from jax import lax
from jax.experimental import pallas as pl
from jax.experimental.pallas import tpu as pltpu
from jax.sharding import PartitionSpec as P

F32 = jnp.float32
BF16 = jnp.bfloat16
VMEM_LIMIT = 56 * 1024 * 1024
LANES = 128


def slot_of(brick_ref, count_ref, s, capacity):
    dest = brick_ref[s]
    rank = jnp.minimum(count_ref[dest], capacity - 1)
    count_ref[dest] = rank + 1
    return dest * capacity + rank


def clear_counts(count_ref):
    def clear(i, _):
        count_ref[i] = 0
        return 0

    lax.fori_loop(0, count_ref.shape[0], clear, 0)


def pack_kernel(pred_ref, pert_ref, out_ref, *, part):
    members, gates, width = pred_ref.shape
    per_tile = LANES // part
    lane = lax.broadcasted_iota(jnp.int32, (gates, LANES), 1) // part
    for which, ref in enumerate((pred_ref, pert_ref)):
        for tile in range(width // LANES):
            blocks = [ref[j, :, tile * LANES : (tile + 1) * LANES] for j in range(members)]
            for q in range(per_tile):
                acc = None
                for j in range(members):
                    shift = ((j - q) * part) % LANES
                    moved = pltpu.roll(blocks[j], shift, 1) if shift else blocks[j]
                    acc = moved if acc is None else jnp.where(lane == j, moved, acc)
                out_ref[tile * per_tile + q, which * gates : (which + 1) * gates, :] = acc.astype(
                    BF16
                )


def taper_kernel(brick_ref, taper_ref, tiles_ref, out_ref, rows_ref, slots_ref, count_ref):
    soundings, length = taper_ref.shape
    bricks = out_ref.shape[0]
    pieces = length // LANES
    rows_ref[...] = jnp.zeros_like(rows_ref)
    slots_ref[...] = jnp.zeros_like(slots_ref)
    for f in range(pieces):
        rows_ref[pl.ds(f, soundings, stride=8), :] = taper_ref[
            :, f * LANES : (f + 1) * LANES
        ].astype(F32)
    numbers = jnp.concatenate(
        [tiles_ref[...].astype(F32), jnp.zeros((LANES - pieces, soundings), F32)], axis=0
    )
    rows_ref[pl.ds(pieces, soundings, stride=8), :] = numbers.T
    capacity = slots_ref.shape[0] // bricks
    clear_counts(count_ref)

    def place(s, _):
        slot = slot_of(brick_ref, count_ref, s, capacity)
        slots_ref[slot] = rows_ref[pl.ds(pl.multiple_of(s * 8, 8), 8), :]
        return 0

    lax.fori_loop(0, soundings, place, 0)
    out_ref[...] = slots_ref[...].reshape(bricks, 8 * capacity, LANES).astype(BF16)


def owner_kernel(
    brick_ref, got_ref, observed_ref, noise_ref, taper_ref, send_ref, wide_ref, turned_ref, count_ref
):
    sources = got_ref.shape[0]
    soundings, gates = observed_ref.shape
    seen_all = observed_ref[...].T
    noise_all = noise_ref[...].T
    rows = 2 * gates
    per_lane = LANES // soundings
    bricks = count_ref.shape[0]
    mems = send_ref.shape[0] // bricks
    block = LANES // mems
    capacity = taper_ref.shape[1] // 8
    filled = capacity * block
    scale = 1.0 / (LANES - 1.0)
    send_ref[:, :filled, :] = jnp.zeros((mems * bricks, filled, LANES), BF16)
    for m in range(mems):
        send_ref[m * bricks : (m + 1) * bricks, filled:, :] = taper_ref[...]
    clear_counts(count_ref)
    wide_ref[...] = got_ref[...].reshape(sources * rows, LANES).astype(F32)
    depth = per_lane * LANES
    r = lax.broadcasted_iota(jnp.int32, (depth, depth), 0)
    c = lax.broadcasted_iota(jnp.int32, (depth, depth), 1)
    want = (c // LANES) * sources + ((c % LANES) // per_lane) + (c % per_lane) * LANES
    select = jnp.where(r == want, 1.0, 0.0).astype(BF16)
    lefts = []
    for group in range(rows // per_lane):
        stack = jnp.concatenate(
            [
                wide_ref[pl.ds(group * per_lane + k, sources, stride=rows), :]
                for k in range(per_lane)
            ],
            axis=0,
        )
        turned = stack.astype(BF16).T
        lefts.append(
            jnp.concatenate(
                [turned[j * soundings : (j + 1) * soundings, :] for j in range(per_lane)], axis=1
            ).astype(BF16)
        )
    left = jnp.concatenate(lefts, axis=0)
    placed = jnp.dot(left, select, preferred_element_type=F32)
    for group in range(rows // per_lane):
        for k in range(per_lane):
            g = group * per_lane + k
            turned_ref[g // gates, pl.ds(g % gates, soundings, stride=gates), :] = placed[
                group * soundings : (group + 1) * soundings, k * LANES : (k + 1) * LANES
            ]
    many = LANES // gates
    count = -(-soundings // many)
    sub8 = lax.broadcasted_iota(jnp.int32, (8, LANES), 0)
    lane8 = lax.broadcasted_iota(jnp.int32, (8, LANES), 1)
    base8 = jnp.minimum(lane8 // gates, many - 1) * gates
    within8 = lane8 - base8
    row = lax.broadcasted_iota(jnp.int32, (gates, LANES), 0)
    lane = lax.broadcasted_iota(jnp.int32, (gates, LANES), 1)
    part = lane // gates
    full = lambda x: jnp.concatenate([x, jnp.zeros((LANES - x.shape[0], LANES), F32)], axis=0)
    anomalies, rights, mats = [], [], []
    for t in range(count):
        here = range(t * many, min(soundings, (t + 1) * many))
        span = slice(t * many * gates, t * many * gates + len(here) * gates)
        pred = turned_ref[0, span, :]
        pert = turned_ref[1, span, :]
        anomaly = full(pred - jnp.sum(pred, axis=1, keepdims=True) * (1.0 / LANES))
        noise = jnp.concatenate([noise_all[:, s : s + 1] for s in here], axis=0)
        observed = jnp.concatenate([seen_all[:, s : s + 1] for s in here], axis=0)
        rights.append(full(observed + noise * pert - pred))
        cov = lax.dot_general(
            anomaly,
            anomaly,
            (((1,), (1,)), ((), ())),
            precision=lax.Precision.HIGHEST,
            preferred_element_type=F32,
        )
        mat = jnp.zeros((gates, LANES), F32)
        for u in range(many):
            at = slice(u * gates, (u + 1) * gates)
            if u < len(here):
                variance = noise[at] * noise[at]
                mine = cov[at] * scale + jnp.where(row + u * gates == lane, variance, 0.0)
            else:
                mine = jnp.where(row + u * gates == lane, 1.0, 0.0)
            mat = jnp.where(part == u, mine, mat)
        anomalies.append(anomaly)
        mats.append([mat[8 * i : 8 * i + 8] for i in range(gates // 8)])
    for k in range(gates):
        index = base8 + k
        at_k = within8 == k
        home, line = divmod(k, 8)
        for t in range(count):
            tiles = mats[t]
            sides = [jnp.take_along_axis(x, index, axis=1) for x in tiles]
            top = jnp.where(at_k, 1.0, tiles[home])[line : line + 1] / sides[home][line : line + 1]
            top = jnp.broadcast_to(top, (8, LANES))
            mats[t] = [
                jnp.where(at_k, 0.0, x) - side * top if i != home
                else jnp.where(sub8 == line, top, jnp.where(at_k, 0.0, x) - side * top)
                for i, (x, side) in enumerate(zip(tiles, sides))
            ]
    for t in range(count):
        here = range(t * many, min(soundings, (t + 1) * many))
        inverse = jnp.concatenate(mats[t], axis=0)
        spread = full(
            jnp.concatenate([jnp.where(part == u, inverse, 0.0) for u in range(many)], axis=0)
        )
        solved = (
            jnp.dot(
                spread, rights[t], precision=lax.Precision.HIGHEST, preferred_element_type=F32
            )
            * scale
        )
        gain = solved.astype(BF16).T
        rounded = anomalies[t].astype(BF16)
        which = lax.broadcasted_iota(jnp.int32, (LANES, LANES), 0) // gates
        right = jnp.concatenate(
            [jnp.where(which == u, rounded, jnp.zeros_like(rounded)) for u in range(len(here))], axis=1
        )
        weight = jnp.dot(gain, right, preferred_element_type=F32).astype(BF16)
        for u, s in enumerate(here):
            slot = slot_of(brick_ref, count_ref, s, capacity)
            first = pl.multiple_of((slot % capacity) * block, block)
            for m in range(mems):
                send_ref[m * bricks + slot // capacity, pl.ds(first, block), :] = weight[
                    m * block : (m + 1) * block, u * LANES : (u + 1) * LANES
                ]


def assemble_kernel(me_ref, *refs):
    parts = refs[:-2]
    out_ref, sems = refs[-2:]
    half = parts[0].shape[0]
    mems = len(parts) // 2
    me = me_ref[0]
    copies = []
    for n, ref in enumerate(parts):
        first = ((me - n // 2) & (mems - 1)) * 2 * half + (n % 2) * half
        first = pl.multiple_of(first, half)
        copies.append(pltpu.make_async_copy(ref, out_ref.at[pl.ds(first, half), :], sems.at[n]))
    for copy in copies:
        copy.start()
    for copy in copies:
        copy.wait()


def update_kernel(
    model_hbm_ref,
    recv_ref,
    members_ref,
    out_ref,
    model_ref,
    taper_ref,
    turn_ref,
    tiles_ref,
    model_sem,
    held_sem,
    table_sem,
    *,
    unit,
    capacity,
    pieces,
):
    sources = recv_ref.shape[0]
    block = members_ref.shape[0]
    filled = capacity * block
    model = pltpu.make_async_copy(model_hbm_ref, model_ref, model_sem)
    held = pltpu.make_async_copy(members_ref, out_ref, held_sem)
    model.start()
    held.start()
    taper_ref[...] = recv_ref[:, filled:, :].astype(F32).reshape(sources * 8 * capacity, LANES)
    for c in range(capacity):
        numbers = taper_ref[pl.ds(8 * c + pieces, sources, stride=8 * capacity), :].T
        turn_ref[c] = numbers[:8, :].astype(jnp.int32)
    table = pltpu.make_async_copy(turn_ref, tiles_ref, table_sem)
    table.start()
    table.wait()
    model.wait()
    held.wait()

    def turn(i, _):
        items = []
        for u in range(unit):
            src = i * unit + u
            for c in range(capacity):
                where = [
                    pl.multiple_of(tiles_ref[c, f, src] * LANES, LANES) for f in range(pieces)
                ]
                items.append((src, c, where))
        rises = []
        for src, c, where in items:
            cells = jnp.concatenate([model_ref[:, pl.ds(at, LANES)] for at in where], axis=1)
            weight = recv_ref[src, c * block : (c + 1) * block, :]
            rises.append(jnp.dot(weight, cells, preferred_element_type=F32))
        for (src, c, where), rise in zip(items, rises):
            rows = pl.multiple_of((src * capacity + c) * 8, 8)
            taper = taper_ref[pl.ds(rows, 8), :]
            for f in range(pieces):
                at = pl.ds(where[f], LANES)
                out_ref[:, at] = (
                    out_ref[:, at] + rise[:, f * LANES : (f + 1) * LANES] * taper[f : f + 1, :]
                )
        return 0

    lax.fori_loop(0, sources // unit, turn, 0)


def params():
    return pltpu.CompilerParams(vmem_limit_bytes=VMEM_LIMIT)


def cost(us):
    return pl.CostEstimate(flops=us * 1000000000, transcendentals=0, bytes_accessed=us * 3000000)


def vmem(n):
    return [pl.BlockSpec(memory_space=pltpu.VMEM)] * n


def smem():
    return pl.BlockSpec(memory_space=pltpu.SMEM)


def body(
    members, predicted, perturbation, observed, noise_std, taper_weights, foot_brick, foot_tiles
):
    mems = lax.axis_size("mem")
    bricks = lax.axis_size("brick")
    devices = mems * bricks
    gates = predicted.shape[1]
    soundings = observed.shape[1]
    ensemble = predicted.shape[0] * bricks
    capacity = 2
    slots = bricks * capacity
    pieces = foot_tiles.shape[1]
    brick = foot_brick[:, 0]
    sds = jax.ShapeDtypeStruct

    def shifted(x, by):
        return lax.ppermute(x, "mem", [(i, (i + by) % mems) for i in range(mems)])

    packed = pl.pallas_call(
        lambda *refs: pack_kernel(*refs, part=soundings),
        out_shape=sds((bricks, 2 * gates, LANES), BF16),
        in_specs=vmem(2),
        out_specs=vmem(1)[0],
        compiler_params=params(),
        cost_estimate=cost(3),
        name="pack",
    )(predicted, perturbation)
    got = lax.all_to_all(packed, "brick", split_axis=0, concat_axis=0, tiled=True)

    held, _ = lax.optimization_barrier((members, packed))
    half = members.shape[0] // 2
    upper, lower = held[:half].astype(BF16), held[half:].astype(BF16)
    upper1, lower3 = shifted(upper, 1), shifted(lower, -1)
    lower1, upper3 = shifted(lower, 1), shifted(upper, -1)

    brick, _ = lax.optimization_barrier((brick, packed))
    taper_rows = pl.pallas_call(
        taper_kernel,
        out_shape=sds((bricks, 8 * capacity, LANES), BF16),
        in_specs=[smem()] + vmem(2),
        out_specs=vmem(1)[0],
        scratch_shapes=[
            pltpu.VMEM((soundings * 8, LANES), F32),
            pltpu.VMEM((slots, 8, LANES), F32),
            pltpu.SMEM((bricks,), jnp.int32),
        ],
        compiler_params=params(),
        cost_estimate=cost(2),
        name="route_taper",
    )(brick, taper_weights, foot_tiles.T)

    got = pltpu.with_memory_space_constraint(got, pltpu.VMEM)
    weight_send = pl.pallas_call(
        owner_kernel,
        out_shape=sds((devices, capacity * (ensemble // mems + 8), ensemble), BF16),
        in_specs=[smem()] + vmem(4),
        out_specs=vmem(1)[0],
        scratch_shapes=[
            pltpu.VMEM((bricks * 2 * gates, LANES), F32),
            pltpu.VMEM((2, soundings * gates, LANES), F32),
            pltpu.SMEM((bricks,), jnp.int32),
        ],
        compiler_params=params(),
        cost_estimate=cost(15),
        name="owner",
    )(brick, got, observed.T, noise_std.T, taper_rows)
    weight_send, upper1, lower1, upper3, lower3 = lax.optimization_barrier(
        (weight_send, upper1, lower1, upper3, lower3)
    )
    upper2, lower2 = shifted(upper1, 1), shifted(lower3, -1)
    halves = (upper, lower, upper1, lower1, upper2, lower2, upper3, lower3)
    weight_recv = lax.all_to_all(
        weight_send, ("mem", "brick"), split_axis=0, concat_axis=0, tiled=True
    )
    me = lax.axis_index("mem").astype(jnp.int32).reshape(1)
    hbm = pl.BlockSpec(memory_space=pl.ANY)
    model_all = pl.pallas_call(
        assemble_kernel,
        out_shape=sds((ensemble, members.shape[1]), BF16),
        in_specs=[smem()] + [hbm] * (2 * mems),
        out_specs=vmem(1)[0],
        scratch_shapes=[pltpu.SemaphoreType.DMA((2 * mems,))],
        compiler_params=params(),
        cost_estimate=cost(40),
        name="assemble",
    )(me, *halves)
    weight_recv = pltpu.with_memory_space_constraint(weight_recv, pltpu.VMEM)
    return pl.pallas_call(
        lambda *refs: update_kernel(*refs, unit=32, capacity=capacity, pieces=pieces),
        out_shape=sds(members.shape, F32),
        in_specs=[hbm] + vmem(1) + [hbm],
        out_specs=vmem(1)[0],
        scratch_shapes=[
            pltpu.VMEM(model_all.shape, BF16),
            pltpu.VMEM((devices * 8 * capacity, LANES), F32),
            pltpu.VMEM((capacity, 8, devices), jnp.int32),
            pltpu.SMEM((capacity, 8, devices), jnp.int32),
            pltpu.SemaphoreType.DMA(()),
            pltpu.SemaphoreType.DMA(()),
            pltpu.SemaphoreType.DMA(()),
        ],
        compiler_params=params(),
        cost_estimate=cost(20),
        name="update",
    )(model_all, weight_recv, members)


def solution(mesh):
    in_specs = (
        P("mem", "brick"),
        P("brick", None, "mem"),
        P("brick", None, "mem"),
        P(None, ("mem", "brick")),
        P(None, ("mem", "brick")),
        P(("mem", "brick"), None),
        P(("mem", "brick"), None),
        P(("mem", "brick"), None),
    )
    out_specs = P("mem", "brick")
    return jax.shard_map(body, mesh=mesh, in_specs=in_specs, out_specs=out_specs, check_vma=False)
```
